32 devices in a mesh: grp: 4 (over z), row: 8 (over y, x, core).
Axes of the slice: x: 2, y: 2, z: 4, core: 2. Of those that a mesh axis runs over, the one named last changes fastest.
Arguments:
- basis: float32 [8192, 1024], P(('grp', 'row')), may hold values from -40 to 40
- block: float32 [8192, 512], P(('grp', 'row')), may hold values from -600 to 600
- counts: int32 [4, 8], P('grp', 'row'), may hold values from 128 to 256, as said below
Outputs:
- new_block: float32 [8192, 512], P(('grp', 'row'))
- factor: float32 [512, 512], replicated
The draws below stay inside these ranges and needn't reach their ends.
Inputs may be any that keep to these rules, and one draw needn't show every extreme that they name: `counts`: each device's live rows are a multiple of 128, at most 256; one device holds exactly 256.
All inputs are finite; a program needn't handle non-finite values.
Results may differ from the reference program's by a relative error of at most 0.0003.
Values sent between devices are 32-bit elements; how exact they have to be, the bound alone decides.
A program may use at most 64 MiB of HBM per device.

```python
import math
import jax
import jax.numpy as jnp
from jax import lax

M = 1024
K = 512
CAP = 256
ROWS_ALL = 8192
N_GRP = 4
N_ROW = 8


def draw_counts(key, part):
    tiles = CAP // 128
    upper = max(2, 2 * tiles // 3)
    base = jax.random.randint(key, (N_GRP * N_ROW,), 1, upper)
    heavy = jax.random.randint(jax.random.fold_in(key, 7), (), 0, N_GRP * N_ROW)
    places = jnp.arange(N_GRP * N_ROW, dtype=jnp.int32)
    filled = jnp.where(places == heavy, tiles, base)
    return (filled * 128).reshape(N_GRP, N_ROW).astype(jnp.int32)


def live_rows(key, part):
    filled = draw_counts(key, part).reshape(-1)
    positions = jnp.arange(ROWS_ALL, dtype=jnp.int32)
    limit = filled[positions // CAP]
    return (positions % CAP < limit).astype(jnp.float32)[:, None]


def basis_span(key, part):
    live = live_rows(key, part)
    raw = jax.random.normal(jax.random.fold_in(key, 101), (ROWS_ALL, M), jnp.float32) * live
    orthonormal, upper_part = jnp.linalg.qr(raw)
    orthonormal = orthonormal * live * math.sqrt(ROWS_ALL)
    tilt = jnp.eye(M, dtype=jnp.float32) + 0.032 * jax.random.normal(jax.random.fold_in(key, 102), (M, M), jnp.float32) / math.sqrt(M)
    spanned = jnp.dot(orthonormal, tilt, precision=lax.Precision.HIGHEST) * live
    return (spanned, live)


def draw_basis(key, part):
    spanned, live = basis_span(key, part)
    filler = 1.7 * jax.random.normal(jax.random.fold_in(key, 103), (ROWS_ALL, M), jnp.float32)
    return jnp.clip(spanned + (1.0 - live) * filler, -40.0, 40.0)


def draw_block(key, part):
    spanned, live = basis_span(key, part)
    amounts = 30.0 * jax.random.normal(jax.random.fold_in(key, 201), (M, K), jnp.float32) / math.sqrt(M)
    along = jnp.dot(spanned, amounts, precision=lax.Precision.HIGHEST)
    rough = jax.random.normal(jax.random.fold_in(key, 202), (ROWS_ALL, K), jnp.float32)
    column_scale = jnp.exp(jax.random.uniform(jax.random.fold_in(key, 203), (K,), jnp.float32, math.log(0.5), math.log(5.0)))
    mixing = jnp.eye(K, dtype=jnp.float32) + 0.3 * jax.random.normal(jax.random.fold_in(key, 204), (K, K), jnp.float32) / math.sqrt(K)
    off_span = jnp.dot(rough * column_scale[None, :], mixing, precision=lax.Precision.HIGHEST)
    filler = jax.random.normal(jax.random.fold_in(key, 205), (ROWS_ALL, K), jnp.float32)
    return jnp.clip(live * (along + off_span) + (1.0 - live) * filler, -600.0, 600.0)


def setup_inputs(seed: int = 0) -> dict:
    seeds = jax.random.split(jax.random.key(seed), 4)
    return {
        "basis": draw_basis(jax.random.fold_in(seeds[3], 71), 0),
        "block": draw_block(jax.random.fold_in(seeds[3], 71), 0),
        "counts": draw_counts(jax.random.fold_in(seeds[3], 71), 0),
    }


def reference(basis, block, counts):
    total = basis.shape[0]
    positions = jnp.arange(total, dtype=jnp.int32)
    owner = positions // CAP
    limit = counts.reshape(-1).astype(jnp.int32)[owner]
    live = (positions % CAP < limit).astype(basis.dtype)[:, None]
    basis_live = basis * live
    block_live = block * live
    coeffs = jnp.dot(basis_live.T, block_live, precision=lax.Precision.HIGHEST) / ROWS_ALL
    first_pass = block_live - jnp.dot(basis_live, coeffs, precision=lax.Precision.HIGHEST)
    correction = jnp.dot(basis_live.T, first_pass, precision=lax.Precision.HIGHEST) / ROWS_ALL
    residual = first_pass - jnp.dot(basis_live, correction, precision=lax.Precision.HIGHEST)
    gram = jnp.dot(residual.T, residual, precision=lax.Precision.HIGHEST) / ROWS_ALL
    lower_factor = jnp.linalg.cholesky(gram)
    new_block = lax.linalg.triangular_solve(lower_factor, residual, left_side=False, lower=True, transpose_a=True)
    return (new_block, lower_factor.T)
```

```python
import functools

import jax
import jax.numpy as jnp
from jax import lax
from jax.experimental import pallas as pl
from jax.experimental.pallas import tpu as pltpu
from jax.sharding import PartitionSpec as P

HIGHEST = lax.Precision.HIGHEST
MESH = pl.DeviceIdType.MESH
TILE = 128


def transposed_product(left, right):
    return lax.dot_general(
        left,
        right,
        (((0,), (0,)), ((), ())),
        precision=HIGHEST,
        preferred_element_type=jnp.float32,
    )


def matrix_product(left, right):
    return jnp.dot(left, right, precision=HIGHEST, preferred_element_type=jnp.float32)


def column_split(rows, cols, first, second):
    split = 1
    while split <= second and cols % (split * TILE) == 0:
        if rows % first == 0 and (rows // first) % (second // split * 8) == 0:
            return split
        split *= 2
    return None


def plan_parts(rows, cols, sizes):
    half = cols // 2
    parts = []
    for start, order in ((0, ("row", "grp")), (half, ("grp", "row"))):
        parts.append((start, half, order, column_split(rows, half, sizes[order[0]], sizes[order[1]])))
    if all(part[3] is not None for part in parts):
        return parts
    order = ("row", "grp")
    split = column_split(rows, cols, sizes["row"], sizes["grp"])
    assert split is not None
    return [(0, cols, order, split)]


def all_reduce_kernel(parts, sizes, x_ref, out_ref, *scratch):
    rows = x_ref.shape[0]
    me = {axis: lax.axis_index(axis) for axis in sizes}

    def ahead(axis, k):
        return lax.rem(me[axis] + k, sizes[axis])

    barrier = pltpu.get_barrier_semaphore()
    for axis in sizes:
        for k in range(1, sizes[axis]):
            pl.semaphore_signal(barrier, inc=1, device_id={axis: ahead(axis, k)}, device_id_type=MESH)
    pl.semaphore_wait(barrier, sum(size - 1 for size in sizes.values()))

    groups = [scratch[7 * i : 7 * i + 7] for i in range(len(parts))]

    def first_chunk(part, index):
        start, width, order, _ = part
        height = rows // sizes[order[0]]
        return pl.ds(pl.multiple_of(index * height, 8), height), pl.ds(start, width)

    def second_chunk(part, index):
        start, width, order, split = part
        height = rows // sizes[order[0]] // (sizes[order[1]] // split)
        piece = width // split
        if split == 1:
            return pl.multiple_of(index * height, 8), height, start, 0, piece
        row = pl.multiple_of(lax.div(index, split) * height, 8)
        offset = pl.multiple_of(lax.rem(index, split) * piece, TILE)
        return row, height, start + offset, offset, piece

    def send(source, target, send_sem, recv_sem, axis, k):
        copy = pltpu.make_async_remote_copy(
            src_ref=source,
            dst_ref=target,
            send_sem=send_sem,
            recv_sem=recv_sem,
            device_id={axis: ahead(axis, k)},
            device_id_type=MESH,
        )
        copy.start()
        return copy

    sent = []
    stage = [[] for _ in parts]
    most = max(sizes.values())
    for k in range(1, most):
        for i, part in enumerate(parts):
            axis = part[2][0]
            if k < sizes[axis]:
                held, _, _, sends, recvs, _, _ = groups[i]
                rs, cs = first_chunk(part, ahead(axis, k))
                stage[i].append(
                    send(x_ref.at[rs, cs], held.at[k - 1], sends.at[k - 1], recvs.at[k - 1], axis, k)
                )
    for i, part in enumerate(parts):
        axis, other = part[2]
        held, partial, held_second, _, _, sends, recvs = groups[i]
        for copy in stage[i]:
            copy.wait_recv()
        rs, cs = first_chunk(part, me[axis])
        total = x_ref[rs, cs]
        for k in range(sizes[axis] - 1):
            total = total + held[k]
        partial[...] = total
        sent += stage[i]
        stage[i] = []
        for k in range(1, sizes[other]):
            row, height, _, offset, piece = second_chunk(part, ahead(other, k))
            stage[i].append(
                send(
                    partial.at[pl.ds(row, height), pl.ds(offset, piece)],
                    held_second.at[k - 1],
                    sends.at[0, k - 1],
                    recvs.at[0, k - 1],
                    other,
                    k,
                )
            )
    for i, part in enumerate(parts):
        axis, other = part[2]
        _, partial, held_second, _, _, sends, recvs = groups[i]
        for copy in stage[i]:
            copy.wait_recv()
        row, height, column, offset, piece = second_chunk(part, me[other])
        total = partial[pl.ds(row, height), pl.ds(offset, piece)]
        for k in range(sizes[other] - 1):
            total = total + held_second[k]
        base = me[axis] * (rows // sizes[axis])
        place = out_ref.at[pl.ds(pl.multiple_of(base + row, 8), height), pl.ds(column, piece)]
        place[...] = total
        sent += stage[i]
        stage[i] = []
        for k in range(1, sizes[other]):
            stage[i].append(send(place, place, sends.at[1, k - 1], recvs.at[1, k - 1], other, k))
    for i, part in enumerate(parts):
        axis, _ = part[2]
        final_sends, final_recvs = scratch[7 * len(parts) + 2 * i : 7 * len(parts) + 2 * i + 2]
        for copy in stage[i]:
            copy.wait_recv()
        sent += stage[i]
        stage[i] = []
        rs, cs = first_chunk(part, me[axis])
        place = out_ref.at[rs, cs]
        for k in range(1, sizes[axis]):
            stage[i].append(send(place, place, final_sends.at[k - 1], final_recvs.at[k - 1], axis, k))
    for i in range(len(parts)):
        for copy in stage[i]:
            copy.wait_recv()
        sent += stage[i]
    for copy in sent:
        copy.wait_send()


def all_reduce(x, collective_id):
    rows, cols = x.shape
    sizes = {axis: lax.axis_size(axis) for axis in ("grp", "row")}
    parts = plan_parts(rows, cols, sizes)
    scratch = []
    for _, width, (axis, other), split in parts:
        height = rows // sizes[axis]
        scratch += [
            pltpu.VMEM((sizes[axis] - 1, height, width), jnp.float32),
            pltpu.VMEM((height, width), jnp.float32),
            pltpu.VMEM((sizes[other] - 1, height // (sizes[other] // split), width // split), jnp.float32),
            pltpu.SemaphoreType.DMA((sizes[axis] - 1,)),
            pltpu.SemaphoreType.DMA((sizes[axis] - 1,)),
            pltpu.SemaphoreType.DMA((2, sizes[other] - 1)),
            pltpu.SemaphoreType.DMA((2, sizes[other] - 1)),
        ]
    for _, _, (axis, _), _ in parts:
        scratch += [pltpu.SemaphoreType.DMA((sizes[axis] - 1,))] * 2
    return pl.pallas_call(
        functools.partial(all_reduce_kernel, parts, sizes),
        out_shape=jax.ShapeDtypeStruct((rows, cols), jnp.float32),
        in_specs=[pl.BlockSpec(memory_space=pltpu.VMEM)],
        out_specs=pl.BlockSpec(memory_space=pltpu.VMEM),
        scratch_shapes=scratch,
        compiler_params=pltpu.CompilerParams(collective_id=collective_id, has_side_effects=True),
        name=f"all_reduce_{collective_id}",
    )(x)


def eliminate(block):
    size = block.shape[0]
    count = size // 8
    sub = lax.broadcasted_iota(jnp.int32, (8, size), 0)
    lane = lax.broadcasted_iota(jnp.int32, (8, size), 1)
    left = [block[8 * b : 8 * b + 8] for b in range(count)]
    right = [(lane == sub + 8 * b).astype(jnp.float32) for b in range(count)]
    for j in range(size):
        home, inner = divmod(j, 8)
        row = left[home][inner : inner + 1]
        companion = right[home][inner : inner + 1]
        inverse = 1.0 / row[:, j : j + 1]
        row = row * inverse
        companion = companion * inverse
        for b in range(home, count):
            if b == home and inner == 7:
                continue
            factor = jnp.broadcast_to(left[b][:, j : j + 1], (8, size))
            if b == home:
                factor = jnp.where(sub > inner, factor, 0.0)
            left[b] = left[b] - factor * row
            right[b] = right[b] - factor * companion
    upper, inverted = [], []
    for b in range(count):
        diagonal = jnp.sum(jnp.where(lane == sub + 8 * b, left[b], 0.0), axis=1, keepdims=True)
        root = 1.0 / jnp.sqrt(diagonal)
        upper.append(jnp.where(lane >= sub + 8 * b, left[b] * root, 0.0))
        inverted.append(jnp.where(lane <= sub + 8 * b, right[b] * root, 0.0))
    return jnp.concatenate(upper, axis=0), jnp.concatenate(inverted, axis=0)


def factor_kernel(gram_ref, residual_ref, new_ref, factor_ref, work, rest):
    size = gram_ref.shape[0]
    work[...] = gram_ref[...]
    rest[...] = residual_ref[...]

    def step(index, carry):
        window = pl.ds(pl.multiple_of(index * TILE, TILE), TILE)
        upper, inverted = eliminate(work[window, window])
        panel = matrix_product(inverted, work[window, :])
        column = lax.broadcasted_iota(jnp.int32, (TILE, size), 1)
        panel = jnp.where(column >= (index + 1) * TILE, panel, 0.0)
        factor_ref[window, :] = panel
        factor_ref[window, window] = upper
        work[...] -= transposed_product(panel, panel)
        solved = lax.dot_general(
            rest[:, window],
            inverted,
            (((1,), (1,)), ((), ())),
            precision=HIGHEST,
            preferred_element_type=jnp.float32,
        )
        new_ref[:, window] = solved
        rest[...] -= matrix_product(solved, panel)
        return carry

    lax.fori_loop(0, size // TILE, step, 0)


def factor_and_solve(gram, residual):
    vmem = pl.BlockSpec(memory_space=pltpu.VMEM)
    return pl.pallas_call(
        factor_kernel,
        out_shape=(
            jax.ShapeDtypeStruct(residual.shape, jnp.float32),
            jax.ShapeDtypeStruct(gram.shape, jnp.float32),
        ),
        in_specs=[vmem, vmem],
        out_specs=(vmem, vmem),
        scratch_shapes=[pltpu.VMEM(gram.shape, jnp.float32), pltpu.VMEM(residual.shape, jnp.float32)],
        name="factor_and_solve",
    )(gram, residual)


def body(basis, block, counts):
    row_slots = block.shape[0]
    devices = lax.axis_size("grp") * lax.axis_size("row")
    weight = 1.0 / (row_slots * devices)
    live = (lax.iota(jnp.int32, row_slots) < counts[0, 0]).astype(jnp.float32)[:, None]
    basis_live = basis * live
    block_live = block * live
    coeffs = all_reduce(transposed_product(basis_live, block_live) * weight, 0)
    first_pass = block_live - matrix_product(basis_live, coeffs)
    correction = all_reduce(transposed_product(basis_live, first_pass) * weight, 1)
    residual = first_pass - matrix_product(basis_live, correction)
    gram = all_reduce(transposed_product(residual, residual) * weight, 2)
    return factor_and_solve(gram, residual)


def solution(mesh):
    placed = (P(("grp", "row"), None), P(("grp", "row"), None), P("grp", "row"))
    return jax.shard_map(
        body, mesh=mesh, in_specs=placed, out_specs=(P(("grp", "row"), None), P()), check_vma=False
    )
```

```python
import functools

import jax
import jax.numpy as jnp
from jax import lax
from jax.experimental import pallas as pl
from jax.experimental.pallas import tpu as pltpu
from jax.sharding import PartitionSpec as P

HIGHEST = lax.Precision.HIGHEST
MESH = pl.DeviceIdType.MESH
TILE = 128


def transposed_product(left, right):
    return lax.dot_general(
        left,
        right,
        (((0,), (0,)), ((), ())),
        precision=HIGHEST,
        preferred_element_type=jnp.float32,
    )


def matrix_product(left, right):
    return jnp.dot(left, right, precision=HIGHEST, preferred_element_type=jnp.float32)


def column_split(rows, cols, first, second):
    split = 1
    while split <= second and cols % (split * TILE) == 0:
        if rows % first == 0 and (rows // first) % (second // split * 8) == 0:
            return split
        split *= 2
    return None


def plan_parts(rows, cols, sizes):
    half = cols // 2
    parts = []
    for start, order in ((0, ("row", "grp")), (half, ("grp", "row"))):
        parts.append((start, half, order, column_split(rows, half, sizes[order[0]], sizes[order[1]])))
    if all(part[3] is not None for part in parts):
        return parts
    order = ("row", "grp")
    split = column_split(rows, cols, sizes["row"], sizes["grp"])
    assert split is not None
    return [(0, cols, order, split)]


def all_reduce_kernel(parts, sizes, x_ref, out_ref, *scratch):
    rows = x_ref.shape[0]
    me = {axis: lax.axis_index(axis) for axis in sizes}

    def ahead(axis, k):
        return lax.rem(me[axis] + k, sizes[axis])

    barrier = pltpu.get_barrier_semaphore()
    for axis in sizes:
        for k in range(1, sizes[axis]):
            pl.semaphore_signal(barrier, inc=1, device_id={axis: ahead(axis, k)}, device_id_type=MESH)
    pl.semaphore_wait(barrier, sum(size - 1 for size in sizes.values()))

    groups = [scratch[7 * i : 7 * i + 7] for i in range(len(parts))]

    def first_chunk(part, index):
        start, width, order, _ = part
        height = rows // sizes[order[0]]
        return pl.ds(pl.multiple_of(index * height, 8), height), pl.ds(start, width)

    def second_chunk(part, index):
        start, width, order, split = part
        height = rows // sizes[order[0]] // (sizes[order[1]] // split)
        piece = width // split
        if split == 1:
            return pl.multiple_of(index * height, 8), height, start, 0, piece
        row = pl.multiple_of(lax.div(index, split) * height, 8)
        offset = pl.multiple_of(lax.rem(index, split) * piece, TILE)
        return row, height, start + offset, offset, piece

    def send(source, target, send_sem, recv_sem, axis, k):
        copy = pltpu.make_async_remote_copy(
            src_ref=source,
            dst_ref=target,
            send_sem=send_sem,
            recv_sem=recv_sem,
            device_id={axis: ahead(axis, k)},
            device_id_type=MESH,
        )
        copy.start()
        return copy

    sent = []
    stage = [[] for _ in parts]
    most = max(sizes.values())
    for k in range(1, most):
        for i, part in enumerate(parts):
            axis = part[2][0]
            if k < sizes[axis]:
                held, _, _, sends, recvs, _, _ = groups[i]
                rs, cs = first_chunk(part, ahead(axis, k))
                stage[i].append(
                    send(x_ref.at[rs, cs], held.at[k - 1], sends.at[k - 1], recvs.at[k - 1], axis, k)
                )
    for i, part in enumerate(parts):
        axis, other = part[2]
        held, partial, held_second, _, _, sends, recvs = groups[i]
        for copy in stage[i]:
            copy.wait_recv()
        rs, cs = first_chunk(part, me[axis])
        total = x_ref[rs, cs]
        for k in range(sizes[axis] - 1):
            total = total + held[k]
        partial[...] = total
        sent += stage[i]
        stage[i] = []
        for k in range(1, sizes[other]):
            row, height, _, offset, piece = second_chunk(part, ahead(other, k))
            stage[i].append(
                send(
                    partial.at[pl.ds(row, height), pl.ds(offset, piece)],
                    held_second.at[k - 1],
                    sends.at[0, k - 1],
                    recvs.at[0, k - 1],
                    other,
                    k,
                )
            )
    for i, part in enumerate(parts):
        axis, other = part[2]
        _, partial, held_second, _, _, sends, recvs = groups[i]
        for copy in stage[i]:
            copy.wait_recv()
        row, height, column, offset, piece = second_chunk(part, me[other])
        total = partial[pl.ds(row, height), pl.ds(offset, piece)]
        for k in range(sizes[other] - 1):
            total = total + held_second[k]
        base = me[axis] * (rows // sizes[axis])
        place = out_ref.at[pl.ds(pl.multiple_of(base + row, 8), height), pl.ds(column, piece)]
        place[...] = total
        sent += stage[i]
        stage[i] = []
        for k in range(1, sizes[other]):
            stage[i].append(send(place, place, sends.at[1, k - 1], recvs.at[1, k - 1], other, k))
    for i, part in enumerate(parts):
        axis, _ = part[2]
        final_sends, final_recvs = scratch[7 * len(parts) + 2 * i : 7 * len(parts) + 2 * i + 2]
        for copy in stage[i]:
            copy.wait_recv()
        sent += stage[i]
        stage[i] = []
        rs, cs = first_chunk(part, me[axis])
        place = out_ref.at[rs, cs]
        for k in range(1, sizes[axis]):
            stage[i].append(send(place, place, final_sends.at[k - 1], final_recvs.at[k - 1], axis, k))
    for i in range(len(parts)):
        for copy in stage[i]:
            copy.wait_recv()
        sent += stage[i]
    for copy in sent:
        copy.wait_send()


def all_reduce(x, collective_id):
    rows, cols = x.shape
    sizes = {axis: lax.axis_size(axis) for axis in ("grp", "row")}
    parts = plan_parts(rows, cols, sizes)
    scratch = []
    for _, width, (axis, other), split in parts:
        height = rows // sizes[axis]
        scratch += [
            pltpu.VMEM((sizes[axis] - 1, height, width), jnp.float32),
            pltpu.VMEM((height, width), jnp.float32),
            pltpu.VMEM((sizes[other] - 1, height // (sizes[other] // split), width // split), jnp.float32),
            pltpu.SemaphoreType.DMA((sizes[axis] - 1,)),
            pltpu.SemaphoreType.DMA((sizes[axis] - 1,)),
            pltpu.SemaphoreType.DMA((2, sizes[other] - 1)),
            pltpu.SemaphoreType.DMA((2, sizes[other] - 1)),
        ]
    for _, _, (axis, _), _ in parts:
        scratch += [pltpu.SemaphoreType.DMA((sizes[axis] - 1,))] * 2
    return pl.pallas_call(
        functools.partial(all_reduce_kernel, parts, sizes),
        out_shape=jax.ShapeDtypeStruct((rows, cols), jnp.float32),
        in_specs=[pl.BlockSpec(memory_space=pltpu.VMEM)],
        out_specs=pl.BlockSpec(memory_space=pltpu.VMEM),
        scratch_shapes=scratch,
        compiler_params=pltpu.CompilerParams(collective_id=collective_id, has_side_effects=True),
        name=f"all_reduce_{collective_id}",
    )(x)


def eliminate(block):
    size = block.shape[0]
    count = size // 8
    sub = lax.broadcasted_iota(jnp.int32, (8, size), 0)
    lane = lax.broadcasted_iota(jnp.int32, (8, size), 1)
    left = [block[8 * b : 8 * b + 8] for b in range(count)]
    right = [(lane == sub + 8 * b).astype(jnp.float32) for b in range(count)]
    for j in range(0, size, 2):
        home, inner = divmod(j, 8)
        row, next_row = left[home][inner : inner + 1], left[home][inner + 1 : inner + 2]
        mate, next_mate = right[home][inner : inner + 1], right[home][inner + 1 : inner + 2]
        inverse = 1.0 / row[:, j : j + 1]
        ratio = row[:, j + 1 : j + 2] * inverse
        pivot = next_row[:, j + 1 : j + 2] - ratio * row[:, j + 1 : j + 2]
        next_inverse = 1.0 / pivot
        next_row = (next_row - ratio * row) * next_inverse
        next_mate = (next_mate - ratio * mate) * next_inverse
        row = row * inverse
        mate = mate * inverse
        for b in range(home, count):
            factor = jnp.broadcast_to(left[b][:, j : j + 1], (8, size))
            next_factor = jnp.broadcast_to(left[b][:, j + 1 : j + 2], (8, size)) - factor * ratio
            if b == home:
                factor = jnp.where(sub > inner, factor, 0.0)
                next_factor = jnp.where(sub > inner + 1, next_factor, 0.0)
            left[b] = left[b] - factor * row - next_factor * next_row
            right[b] = right[b] - factor * mate - next_factor * next_mate
    upper, inverted = [], []
    for b in range(count):
        diagonal = jnp.sum(jnp.where(lane == sub + 8 * b, left[b], 0.0), axis=1, keepdims=True)
        root = 1.0 / jnp.sqrt(diagonal)
        upper.append(jnp.where(lane >= sub + 8 * b, left[b] * root, 0.0))
        inverted.append(jnp.where(lane <= sub + 8 * b, right[b] * root, 0.0))
    return jnp.concatenate(upper, axis=0), jnp.concatenate(inverted, axis=0)


def factor_kernel(gram_ref, residual_ref, new_ref, factor_ref, work, rest):
    size = gram_ref.shape[0]
    work[...] = gram_ref[...]
    rest[...] = residual_ref[...]

    def step(index, carry):
        window = pl.ds(pl.multiple_of(index * TILE, TILE), TILE)
        upper, inverted = eliminate(work[window, window])
        panel = matrix_product(inverted, work[window, :])
        column = lax.broadcasted_iota(jnp.int32, (TILE, size), 1)
        panel = jnp.where(column >= (index + 1) * TILE, panel, 0.0)
        factor_ref[window, :] = panel
        factor_ref[window, window] = upper
        work[...] -= transposed_product(panel, panel)
        solved = lax.dot_general(
            rest[:, window],
            inverted,
            (((1,), (1,)), ((), ())),
            precision=HIGHEST,
            preferred_element_type=jnp.float32,
        )
        new_ref[:, window] = solved
        rest[...] -= matrix_product(solved, panel)
        return carry

    lax.fori_loop(0, size // TILE, step, 0)


def factor_and_solve(gram, residual):
    vmem = pl.BlockSpec(memory_space=pltpu.VMEM)
    return pl.pallas_call(
        factor_kernel,
        out_shape=(
            jax.ShapeDtypeStruct(residual.shape, jnp.float32),
            jax.ShapeDtypeStruct(gram.shape, jnp.float32),
        ),
        in_specs=[vmem, vmem],
        out_specs=(vmem, vmem),
        scratch_shapes=[pltpu.VMEM(gram.shape, jnp.float32), pltpu.VMEM(residual.shape, jnp.float32)],
        name="factor_and_solve",
    )(gram, residual)


def body(basis, block, counts):
    row_slots = block.shape[0]
    devices = lax.axis_size("grp") * lax.axis_size("row")
    weight = 1.0 / (row_slots * devices)
    live = (lax.iota(jnp.int32, row_slots) < counts[0, 0]).astype(jnp.float32)[:, None]
    basis_live = basis * live
    block_live = block * live
    coeffs = all_reduce(transposed_product(basis_live, block_live) * weight, 0)
    first_pass = block_live - matrix_product(basis_live, coeffs)
    correction = all_reduce(transposed_product(basis_live, first_pass) * weight, 1)
    residual = first_pass - matrix_product(basis_live, correction)
    gram = all_reduce(transposed_product(residual, residual) * weight, 2)
    return factor_and_solve(gram, residual)


def solution(mesh):
    placed = (P(("grp", "row"), None), P(("grp", "row"), None), P("grp", "row"))
    return jax.shard_map(
        body, mesh=mesh, in_specs=placed, out_specs=(P(("grp", "row"), None), P()), check_vma=False
    )
```
